32 devices in a mesh: ka: 4 (over y, x), pw: 8 (over z, core).
Axes of the slice: x: 2, y: 2, z: 4, core: 2. Of those that a mesh axis runs over, the one named last changes fastest.
Arguments:
- band_coeffs: bfloat16 [4, 2, 1024, 384], P('ka', None, 'pw'), may hold values from -6 to 6
- cutoff_weight: float32 [4, 1024], P('ka', 'pw'), may hold values from 0.3 to 3
- row_order: int32 [4, 1024], P('ka', 'pw'), may hold values from 0 to 1023, as said below
- neighbour: int32 [4], P('ka'), may hold values from 0 to 3, as said below
- gauge_matrix: bfloat16 [4, 2, 384, 384], P('ka'), may hold values from -0.21875 to 0.21875
Outputs:
- whitened: bfloat16 [4, 2, 1024, 384], P('ka', None, 'pw')
- correlations: float32 [4, 2, 2, 384, 384], P('ka')
The draws below stay inside these ranges and needn't reach their ends.
Inputs may be any that keep to these rules, and one draw needn't show every extreme that they name: `row_order`: within each aligned block of 128 entries of a row, the entries are a permutation of that block's own indices. neighbour[k] is (k + 1) mod 4 or (k - 1) mod 4; groups 0 and 1 take the second.
All inputs are finite; a program needn't handle non-finite values.
Results may differ from the reference program's by a relative error of at most 0.009.
Values may be sent and summed in bfloat16 or wider, within the bound.
A program may use at most 64 MiB of HBM per device.

```python
import math
import jax
import jax.numpy as jnp
from jax import lax

NB = 384
PW_DEV = 128
NS_STEPS = 2
NK = 4
NPW = 1024


def draw_band_coeffs(key, part):
    shape = (NK, 2, NPW, NB)
    values = jnp.clip(jax.random.normal(jax.random.fold_in(key, 41), shape, jnp.float32), -6.0, 6.0)
    return values.astype(jnp.bfloat16)


def draw_row_order(key, part):
    block_count = NK * (NPW // PW_DEV)
    subkeys = jax.random.split(jax.random.fold_in(key, 11), block_count)
    orders = jax.vmap(lambda sub_key: jax.random.permutation(sub_key, PW_DEV))(subkeys)
    offsets = jnp.arange(block_count, dtype=jnp.int32) % (NPW // PW_DEV) * PW_DEV
    return (orders.astype(jnp.int32) + offsets[:, None]).reshape(NK, NPW)


def draw_neighbour(key, part):
    signs = jax.random.randint(jax.random.fold_in(key, 23), (NK,), 0, 2).astype(jnp.int32) * 2 - 1
    positions = jnp.arange(NK, dtype=jnp.int32)
    signs = jnp.where(positions < 2, -1, signs)
    return ((positions + signs + NK) % NK).astype(jnp.int32)


def level_of(own_key, dims, pieces, least, largest):
    def one(dim, shards_of):
        heights = jax.random.uniform(jax.random.fold_in(jax.random.fold_in(own_key, 6), dim), (shards_of,), jnp.float32, least / len(pieces), largest / len(pieces))
        return jnp.repeat(jnp.exp(heights), dims[dim] // shards_of).reshape((-1,) + (1,) * (len(dims) - dim - 1))

    level = one(*pieces[0])
    for cut in pieces[1:]:
        level = level * one(*cut)
    return level


def scatter_about(own_key, shape, spread, bound, cuts=(), held_as=jnp.bfloat16):
    entries = jax.random.normal(own_key, shape, jnp.float32) * spread
    if len(cuts) > 0:
        entries = level_of(own_key, shape, cuts, -0.22, 0.18) * entries
    return jnp.clip(entries, min=-bound, max=bound).astype(held_as)


def setup_inputs(seed: int = 0) -> dict:
    streams_of = jax.random.split(jax.random.key(seed), 6)
    return {
        "band_coeffs": draw_band_coeffs(jax.random.fold_in(streams_of[5], 71), 0),
        "cutoff_weight": jnp.clip(jnp.exp(math.log(3.0) - 2.3025851 * jax.random.uniform(streams_of[1], (NK, NPW), jnp.float32) ** level_of(streams_of[1], (NK, NPW), ((0, 4), (1, 8)), -0.2, 0.2)), 0.3, 3.0),
        "row_order": draw_row_order(jax.random.fold_in(streams_of[5], 71), 0),
        "neighbour": draw_neighbour(jax.random.fold_in(streams_of[5], 71), 0),
        "gauge_matrix": scatter_about(streams_of[4], (NK, 2, NB, NB), (2 * NB) ** -0.5, 0.21875, ((0, 4),)),
    }


def precise_dot(left, right):
    return jnp.dot(left, right, precision=lax.Precision.HIGHEST, preferred_element_type=jnp.float32)

def complex_product(left_re, left_im, right_re, right_im):
    real_part = precise_dot(left_re, right_re) - precise_dot(left_im, right_im)
    imag_part = precise_dot(left_re, right_im) + precise_dot(left_im, right_re)
    return (real_part, imag_part)

def lowered_dot(left, right):
    return jnp.dot(left, right, preferred_element_type=jnp.float32)

def whitening(gram_re, gram_im, scale):
    identity = jnp.eye(gram_re.shape[0], dtype=jnp.float32)
    upper_re = gram_re / scale
    upper_im = gram_im / scale
    lower_re = identity
    lower_im = jnp.zeros_like(identity)
    for ns_turn in range(NS_STEPS):
        prod_re, prod_im = complex_product(lower_re, lower_im, upper_re, upper_im)
        middle_re = 1.5 * identity - 0.5 * prod_re
        middle_im = -0.5 * prod_im
        upper_re, upper_im = complex_product(upper_re, upper_im, middle_re, middle_im)
        lower_re, lower_im = complex_product(middle_re, middle_im, lower_re, lower_im)
    return (lower_re, lower_im)

def apply_whitening(filtered, white_re, white_im):
    wide_re = white_re.astype(jnp.bfloat16)
    wide_im = white_im.astype(jnp.bfloat16)
    out_re = lowered_dot(filtered[0], wide_re) - lowered_dot(filtered[1], wide_im)
    out_im = lowered_dot(filtered[0], wide_im) + lowered_dot(filtered[1], wide_re)
    return jnp.stack([out_re, out_im]).astype(jnp.bfloat16)

def rotate(mix_re, mix_im, own_gauge, next_gauge):
    rot_re = (lowered_dot(mix_re, next_gauge[0]) - lowered_dot(mix_im, next_gauge[1])).astype(jnp.bfloat16)
    rot_im = (lowered_dot(mix_re, next_gauge[1]) + lowered_dot(mix_im, next_gauge[0])).astype(jnp.bfloat16)
    out_re = lowered_dot(own_gauge[0].T, rot_re) + lowered_dot(own_gauge[1].T, rot_im)
    out_im = lowered_dot(own_gauge[0].T, rot_im) - lowered_dot(own_gauge[1].T, rot_re)
    return jnp.stack([out_re, out_im])

def reference(band_coeffs, cutoff_weight, row_order, neighbour, gauge_matrix):
    filtered = (band_coeffs.astype(jnp.float32) * cutoff_weight[:, None, :, None]).astype(jnp.bfloat16)

    def whiten_group(group):
        wide = group.astype(jnp.float32)
        blocks = jnp.einsum('prn,qrm->pqnm', wide, wide, precision=lax.Precision.HIGHEST)
        gram_re = blocks[0, 0] + blocks[1, 1]
        gram_im = blocks[0, 1] - blocks[1, 0]
        scale = 2.0 * jnp.sum(wide * wide) / NB
        white_re, white_im = whitening(gram_re, gram_im, scale)
        return apply_whitening(group, white_re, white_im)
    whitened = lax.map(whiten_group, filtered)
    root_scale = jnp.sqrt(jnp.float32(NPW))

    def one_direction(group_index, partner_index):
        own = whitened[group_index].astype(jnp.float32)
        other = whitened[partner_index]
        moved = jnp.take(other, row_order[group_index].astype(jnp.int32), axis=1).astype(jnp.float32)
        blocks = jnp.einsum('prn,qrm->pqnm', own, moved, precision=lax.Precision.HIGHEST)
        mix_re = ((blocks[0, 0] + blocks[1, 1]) * root_scale).astype(jnp.bfloat16)
        mix_im = ((blocks[0, 1] - blocks[1, 0]) * root_scale).astype(jnp.bfloat16)
        return rotate(mix_re, mix_im, gauge_matrix[group_index], gauge_matrix[partner_index])

    def correlation_group(group_index):
        first = neighbour[group_index].astype(jnp.int32)
        second = ((2 * group_index - first + 2 * NK) % NK).astype(jnp.int32)
        return jnp.stack([one_direction(group_index, first), one_direction(group_index, second)])
    correlations = lax.map(correlation_group, jnp.arange(NK, dtype=jnp.int32))
    return (whitened, correlations)
```

```python
import functools
import math

import jax
import jax.numpy as jnp
from jax import lax
from jax.experimental import pallas as pl
from jax.experimental.pallas import tpu as pltpu
from jax.sharding import PartitionSpec as P

MESH = pl.DeviceIdType.MESH
CORES = 2
A_CHUNKS = 4
F32 = jnp.float32
BF16 = jnp.bfloat16


def mm(left, right):
    return jnp.dot(left, right, preferred_element_type=F32)


def mm_t(left, right):
    return lax.dot_general(left, right, (((0,), (0,)), ((), ())), preferred_element_type=F32)


def complex_mm(left_re, left_im, right_re, right_im):
    real_part = mm(left_re, right_re) - mm(left_im, right_im)
    imag_part = mm(left_re, right_im) + mm(left_im, right_re)
    return real_part, imag_part


def halves(packed):
    turned = packed.T
    return 0.5 * (packed + turned), 0.5 * (packed - turned)


def kernel(
    ka_count,
    pw_count,
    bands_ref,
    weight_ref,
    order_ref,
    gauge_ref,
    white_out,
    corr_out,
    f_buf,
    p_buf,
    fn_buf,
    un_buf,
    a_full,
    local,
    r_buf,
    l_buf,
    s_buf,
    t_buf,
    a_other,
    w_buf,
    wn_buf,
    v_buf,
    c_buf,
    pair_send,
    pair_recv,
    near_send,
    fn_recv,
    un_recv,
    wn_recv,
    red_send,
    red_recv_r,
    red_recv_l,
    tot_recv,
    cast_send,
):
    rows, nb = bands_ref.shape[1], bands_ref.shape[2]
    half = nb // CORES
    chunk = half // A_CHUNKS
    c_chunks = nb // chunk
    pairs_a = A_CHUNKS // 2
    pairs_all = (A_CHUNKS + 2 * c_chunks) // 2
    k = lax.axis_index("ka")
    p = lax.axis_index("pw")
    core = lax.rem(p, CORES)
    q = lax.div(p, CORES)
    line = pw_count // CORES
    low = (line - 1) // 2
    ahead = lax.rem(k + 1, ka_count)
    behind = lax.rem(k + ka_count - 1, ka_count)
    base = q * CORES
    partner = base + 1 - core

    barrier = pltpu.get_barrier_semaphore()

    def greet(a, b):
        pl.semaphore_signal(barrier, inc=1, device_id=(a, b), device_id_type=MESH)

    greet(k, partner)
    for other in (ahead, behind):
        for side in range(CORES):
            greet(other, base + side)

    @pl.when(q > 0)
    def _():
        greet(k, p - CORES)

    @pl.when(q < line - 1)
    def _():
        greet(k, p + CORES)

    row_id = lax.broadcasted_iota(jnp.int32, (rows, rows), 0)
    col_id = lax.broadcasted_iota(jnp.int32, (rows, rows), 1)
    weight = jnp.sum(jnp.where(row_id == col_id, weight_ref[...], 0.0), axis=1, keepdims=True)
    pick = (row_id == order_ref[...] - p * rows).astype(BF16)
    for part in range(2):
        filtered = (bands_ref[part].astype(F32) * weight).astype(BF16)
        f_buf[part] = filtered
        p_buf[core, part] = mm(pick, filtered).astype(BF16)

    @pl.when(q == 0)
    def _():
        r_buf[...] = jnp.zeros_like(r_buf)

    @pl.when(q == line - 1)
    def _():
        l_buf[...] = jnp.zeros_like(l_buf)

    pl.semaphore_wait(barrier, 5 + (q > 0).astype(jnp.int32) + (q < line - 1).astype(jnp.int32))

    def remote(src, dst, send, recv, a, b):
        return pltpu.make_async_remote_copy(
            src_ref=src, dst_ref=dst, send_sem=send, recv_sem=recv,
            device_id=(a, b), device_id_type=MESH,
        )

    def to_pair(src, dst, turn):
        return remote(src, dst, pair_send.at[turn], pair_recv.at[turn], k, partner)

    def to_near(src, dst, recv, turn):
        return (
            remote(src, dst, near_send.at[turn, 0], recv, behind, base),
            remote(src, dst, near_send.at[turn, 1], recv, ahead, base + 1),
        )

    def from_near(buf, recv, turn):
        for side in range(CORES):
            remote(buf.at[side], buf.at[side], near_send.at[turn, 0], recv.at[side], k, partner).wait_recv()

    p_copy = to_pair(p_buf.at[core], p_buf.at[core], 0)
    p_copy.start()
    f_copies = to_near(f_buf, fn_buf.at[core], fn_recv.at[core], 0)
    u_copies = to_near(gauge_ref.at[core], un_buf.at[core], un_recv.at[core], 1)
    for copy in f_copies + u_copies:
        copy.start()

    def got_pair(dst, turn):
        remote(dst, dst, pair_send.at[turn], pair_recv.at[turn], k, partner).wait_recv()

    got_pair(p_buf.at[1 - core], 0)

    def stacked(buf):
        flat = buf[...].reshape(CORES * 2 * rows, nb)
        turned = []
        for side in range(CORES):
            turned += [buf[side, 1], -buf[side, 0]]
        return flat, jnp.concatenate(turned, axis=0)

    own_flat, own_turned = stacked(p_buf)
    a_full[...] = mm_t(own_flat, own_flat) + mm_t(own_flat, own_turned)
    for i in range(A_CHUNKS):
        local[i] = a_full[pl.ds(pl.multiple_of(core * half + i * chunk, 8), chunk), :]

    def reduce_one(i):
        owner = low + lax.rem(i, 2) if line > 1 else 0

        @pl.when(q < owner)
        def _():
            @pl.when(q > 0)
            def _():
                remote(r_buf.at[i], r_buf.at[i], red_send.at[i], red_recv_r.at[i], k, partner).wait_recv()

            s_buf[i] = (local[i] + r_buf[i].astype(F32)).astype(BF16)
            remote(s_buf.at[i], r_buf.at[i], red_send.at[i], red_recv_r.at[i], k, p + CORES).start()

        @pl.when(q > owner)
        def _():
            @pl.when(q < line - 1)
            def _():
                remote(l_buf.at[i], l_buf.at[i], red_send.at[i], red_recv_l.at[i], k, partner).wait_recv()

            s_buf[i] = (local[i] + l_buf[i].astype(F32)).astype(BF16)
            remote(s_buf.at[i], l_buf.at[i], red_send.at[i], red_recv_l.at[i], k, p - CORES).start()

        @pl.when(q == owner)
        def _():
            @pl.when(q > 0)
            def _():
                remote(r_buf.at[i], r_buf.at[i], red_send.at[i], red_recv_r.at[i], k, partner).wait_recv()

            @pl.when(q < line - 1)
            def _():
                remote(l_buf.at[i], l_buf.at[i], red_send.at[i], red_recv_l.at[i], k, partner).wait_recv()

            t_buf[i] = (local[i] + r_buf[i].astype(F32) + l_buf[i].astype(F32)).astype(BF16)

            @pl.when(q > 0)
            def _():
                remote(t_buf.at[i], t_buf.at[i], cast_send.at[0, i], tot_recv.at[i], k, p - CORES).start()

            @pl.when(q < line - 1)
            def _():
                remote(t_buf.at[i], t_buf.at[i], cast_send.at[1, i], tot_recv.at[i], k, p + CORES).start()

    def cast_one(i):
        owner = low + lax.rem(i, 2) if line > 1 else 0

        @pl.when(q != owner)
        def _():
            remote(t_buf.at[i], t_buf.at[i], cast_send.at[0, i], tot_recv.at[i], k, partner).wait_recv()

        @pl.when((q < owner) & (q > 0))
        def _():
            remote(t_buf.at[i], t_buf.at[i], cast_send.at[0, i], tot_recv.at[i], k, p - CORES).start()

        @pl.when((q > owner) & (q < line - 1))
        def _():
            remote(t_buf.at[i], t_buf.at[i], cast_send.at[1, i], tot_recv.at[i], k, p + CORES).start()

    def settle_one(i):
        owner = low + lax.rem(i, 2) if line > 1 else 0

        @pl.when(q != owner)
        def _():
            remote(s_buf.at[i], s_buf.at[i], red_send.at[i], tot_recv.at[i], k, partner).wait_send()

        @pl.when((q <= owner) & (q > 0))
        def _():
            remote(t_buf.at[i], t_buf.at[i], cast_send.at[0, i], tot_recv.at[i], k, partner).wait_send()

        @pl.when((q >= owner) & (q < line - 1))
        def _():
            remote(t_buf.at[i], t_buf.at[i], cast_send.at[1, i], tot_recv.at[i], k, partner).wait_send()

    at_low = (q <= low).astype(jnp.int32)

    def over_pairs(one, first, last):
        def step(j, carry):
            one(2 * j + at_low)
            one(2 * j + 1 - at_low)
            return carry

        lax.fori_loop(first, last, step, 0)

    over_pairs(reduce_one, 0, pairs_a)
    over_pairs(cast_one, 0, pairs_a)

    mine = pl.ds(0, A_CHUNKS)
    a_copy = to_pair(t_buf.at[mine], a_other, 1)
    a_copy.start()

    from_near(fn_buf, fn_recv, 0)
    near_flat, near_turned = stacked(fn_buf)
    local[A_CHUNKS : A_CHUNKS + c_chunks] = mm_t(own_flat, near_flat).reshape(c_chunks, chunk, nb)
    local[A_CHUNKS + c_chunks :] = mm_t(own_flat, near_turned).reshape(c_chunks, chunk, nb)

    outer = (q == 0) | (q == line - 1)

    @pl.when(outer)
    def _():
        over_pairs(reduce_one, pairs_a, pairs_all)

    got_pair(a_other, 1)
    a_full[pl.ds(pl.multiple_of(core * half, 8), half), :] = (
        t_buf[mine].astype(F32).reshape(half, nb)
    )
    a_full[pl.ds(pl.multiple_of((1 - core) * half, 8), half), :] = (
        a_other[...].astype(F32).reshape(half, nb)
    )

    eye = (
        lax.broadcasted_iota(jnp.int32, (nb, nb), 0) == lax.broadcasted_iota(jnp.int32, (nb, nb), 1)
    ).astype(F32)
    packed = a_full[...]
    scale = 2.0 * jnp.sum(packed * eye) / nb
    y_re, y_im = halves(packed / scale)
    y_re_b, y_im_b = y_re.astype(BF16), y_im.astype(BF16)
    sq_re, sq_im = complex_mm(y_re_b, y_im_b, y_re_b, y_im_b)
    left_re = (1.5 * y_re - 0.5 * sq_re).astype(BF16)
    left_im = (1.5 * y_im - 0.5 * sq_im).astype(BF16)
    right_re = (2.25 * eye - 1.5 * y_re + 0.25 * sq_re).astype(BF16)
    right_im = (0.25 * sq_im - 1.5 * y_im).astype(BF16)
    last_re, last_im = complex_mm(left_re, left_im, right_re, right_im)
    white_re = 2.25 * eye - 0.75 * y_re - 0.5 * last_re
    white_im = -0.75 * y_im - 0.5 * last_im
    w_buf[...] = (white_re + white_im).astype(BF16).reshape(CORES, half, nb)
    w_copies = to_near(w_buf.at[core], wn_buf.at[core], wn_recv.at[core], 2)
    for copy in w_copies:
        copy.start()
    w_re, w_im = white_re.astype(BF16), white_im.astype(BF16)

    @pl.when(jnp.logical_not(outer))
    def _():
        over_pairs(reduce_one, pairs_a, pairs_all)

    out_re, out_im = complex_mm(f_buf[0], f_buf[1], w_re, w_im)
    white_out[0] = out_re.astype(BF16)
    white_out[1] = out_im.astype(BF16)
    v_re, v_im = complex_mm(w_re, w_im, gauge_ref[0], gauge_ref[1])
    v_buf[0] = v_re.astype(BF16)
    v_buf[1] = v_im.astype(BF16)

    over_pairs(cast_one, pairs_a, pairs_all)
    from_near(un_buf, un_recv, 1)
    from_near(wn_buf, wn_recv, 2)
    next_re, next_im = halves(wn_buf[...].astype(F32).reshape(nb, nb))
    vn_re, vn_im = complex_mm(next_re.astype(BF16), next_im.astype(BF16), un_buf[0], un_buf[1])
    cross_re = t_buf[A_CHUNKS : A_CHUNKS + c_chunks].reshape(nb, nb)
    cross_im = t_buf[A_CHUNKS + c_chunks :].reshape(nb, nb)
    x_re, x_im = complex_mm(cross_re, cross_im, vn_re.astype(BF16), vn_im.astype(BF16))
    x_re, x_im = x_re.astype(BF16), x_im.astype(BF16)
    root = math.sqrt(rows * pw_count)
    corr_re = mm_t(v_buf[0], x_re) + mm_t(v_buf[1], x_im)
    corr_im = mm_t(v_buf[0], x_im) - mm_t(v_buf[1], x_re)
    c_buf[core, 0] = (corr_re * root).astype(BF16)
    c_buf[core, 1] = (corr_im * root).astype(BF16)
    c_copy = to_pair(c_buf.at[core], c_buf.at[core], 2)
    c_copy.start()

    for copy in (p_copy, a_copy) + f_copies + u_copies + w_copies:
        copy.wait_send()

    def settle(i, carry):
        settle_one(i)
        return carry

    lax.fori_loop(0, 2 * pairs_all, settle, 0)
    got_pair(c_buf.at[1 - core], 2)
    corr_out[...] = c_buf[...]
    c_copy.wait_send()


def on_device(ka_count, pw_count, band_coeffs, cutoff_weight, row_order, neighbour, gauge_matrix):
    rows, nb = band_coeffs.shape[2], band_coeffs.shape[3]
    half = nb // CORES
    chunk = half // A_CHUNKS
    total = A_CHUNKS + 2 * (nb // chunk)
    vmem = pl.BlockSpec(memory_space=pltpu.VMEM)
    dma = pltpu.SemaphoreType.DMA
    whitened, pair = pl.pallas_call(
        functools.partial(kernel, ka_count, pw_count),
        out_shape=(
            jax.ShapeDtypeStruct((2, rows, nb), BF16),
            jax.ShapeDtypeStruct((2, 2, nb, nb), BF16),
        ),
        in_specs=[vmem] * 4,
        out_specs=(vmem, vmem),
        scratch_shapes=[
            pltpu.VMEM((2, rows, nb), BF16),
            pltpu.VMEM((CORES, 2, rows, nb), BF16),
            pltpu.VMEM((CORES, 2, rows, nb), BF16),
            pltpu.VMEM((2, nb, nb), BF16),
            pltpu.VMEM((nb, nb), F32),
            pltpu.VMEM((total, chunk, nb), F32),
            pltpu.VMEM((total, chunk, nb), BF16),
            pltpu.VMEM((total, chunk, nb), BF16),
            pltpu.VMEM((total, chunk, nb), BF16),
            pltpu.VMEM((total, chunk, nb), BF16),
            pltpu.VMEM((A_CHUNKS, chunk, nb), BF16),
            pltpu.VMEM((CORES, half, nb), BF16),
            pltpu.VMEM((CORES, half, nb), BF16),
            pltpu.VMEM((2, nb, nb), BF16),
            pltpu.VMEM((2, 2, nb, nb), BF16),
            dma((3,)),
            dma((3,)),
            dma((3, 2)),
            dma((2,)),
            dma((2,)),
            dma((2,)),
            dma((total,)),
            dma((total,)),
            dma((total,)),
            dma((total,)),
            dma((2, total)),
        ],
        compiler_params=pltpu.CompilerParams(collective_id=0, has_side_effects=True),
    )(band_coeffs[0], cutoff_weight, row_order, gauge_matrix[0])
    group = lax.axis_index("ka")
    looks_ahead = neighbour[0] == (group + 1) % ka_count
    correlations = jnp.where(looks_ahead, pair, pair[::-1]).astype(F32)
    return (whitened[None], correlations[None])


def solution(mesh):
    in_specs = (
        P("ka", None, "pw", None),
        P("ka", "pw"),
        P("ka", "pw"),
        P("ka"),
        P("ka", None, None, None),
    )
    out_specs = (P("ka", None, "pw", None), P("ka", None, None, None, None))
    return jax.shard_map(
        functools.partial(on_device, mesh.shape["ka"], mesh.shape["pw"]),
        mesh=mesh, in_specs=in_specs, out_specs=out_specs, check_vma=False,
    )
```

```python
import functools
import math

import jax
import jax.numpy as jnp
from jax import lax
from jax.experimental import pallas as pl
from jax.experimental.pallas import tpu as pltpu
from jax.sharding import PartitionSpec as P

MESH = pl.DeviceIdType.MESH
CORES = 2
A_CHUNKS = 4
EARLY = 1
TOTAL_LAG = 3
CAST_LAG = 6
F32 = jnp.float32
BF16 = jnp.bfloat16


def mm(left, right):
    return jnp.dot(left, right, preferred_element_type=F32)


def mm_t(left, right):
    return lax.dot_general(left, right, (((0,), (0,)), ((), ())), preferred_element_type=F32)


def complex_mm(left_re, left_im, right_re, right_im):
    real_part = mm(left_re, right_re) - mm(left_im, right_im)
    imag_part = mm(left_re, right_im) + mm(left_im, right_re)
    return real_part, imag_part


def halves(packed):
    turned = packed.T
    return 0.5 * (packed + turned), 0.5 * (packed - turned)


def kernel(
    ka_count,
    pw_count,
    bands_ref,
    weight_ref,
    order_ref,
    gauge_ref,
    white_out,
    corr_out,
    f_buf,
    p_buf,
    fn_buf,
    un_buf,
    a_full,
    local,
    r_buf,
    l_buf,
    s_buf,
    t_buf,
    a_other,
    w_buf,
    wn_buf,
    v_buf,
    c_buf,
    pair_send,
    pair_recv,
    near_send,
    fn_recv,
    un_recv,
    wn_recv,
    red_send,
    red_recv_r,
    red_recv_l,
    tot_recv,
    cast_send,
):
    rows, nb = bands_ref.shape[1], bands_ref.shape[2]
    half = nb // CORES
    chunk = half // A_CHUNKS
    c_chunks = nb // chunk
    pairs_a = A_CHUNKS // 2
    pairs_all = (A_CHUNKS + 2 * c_chunks) // 2
    early = pairs_a + EARLY
    k = lax.axis_index("ka")
    p = lax.axis_index("pw")
    core = lax.rem(p, CORES)
    q = lax.div(p, CORES)
    line = pw_count // CORES
    low = (line - 1) // 2
    ahead = lax.rem(k + 1, ka_count)
    behind = lax.rem(k + ka_count - 1, ka_count)
    base = q * CORES
    partner = base + 1 - core

    barrier = pltpu.get_barrier_semaphore()

    def greet(a, b):
        pl.semaphore_signal(barrier, inc=1, device_id=(a, b), device_id_type=MESH)

    greet(k, partner)
    for other in (ahead, behind):
        for side in range(CORES):
            greet(other, base + side)

    @pl.when(q > 0)
    def _():
        greet(k, p - CORES)

    @pl.when(q < line - 1)
    def _():
        greet(k, p + CORES)

    row_id = lax.broadcasted_iota(jnp.int32, (rows, rows), 0)
    col_id = lax.broadcasted_iota(jnp.int32, (rows, rows), 1)
    weight = jnp.sum(jnp.where(row_id == col_id, weight_ref[...], 0.0), axis=1, keepdims=True)
    pick = (row_id == order_ref[...] - p * rows).astype(BF16)
    for part in range(2):
        filtered = (bands_ref[part].astype(F32) * weight).astype(BF16)
        f_buf[part] = filtered
        p_buf[core, part] = mm(pick, filtered).astype(BF16)

    @pl.when(q == 0)
    def _():
        r_buf[...] = jnp.zeros_like(r_buf)

    @pl.when(q == line - 1)
    def _():
        l_buf[...] = jnp.zeros_like(l_buf)

    pl.semaphore_wait(barrier, 5 + (q > 0).astype(jnp.int32) + (q < line - 1).astype(jnp.int32))

    def remote(src, dst, send, recv, a, b):
        return pltpu.make_async_remote_copy(
            src_ref=src, dst_ref=dst, send_sem=send, recv_sem=recv,
            device_id=(a, b), device_id_type=MESH,
        )

    def to_pair(src, dst, turn):
        return remote(src, dst, pair_send.at[turn], pair_recv.at[turn], k, partner)

    def to_near(src, dst, recv, turn):
        return (
            remote(src, dst, near_send.at[turn, 0], recv, behind, base),
            remote(src, dst, near_send.at[turn, 1], recv, ahead, base + 1),
        )

    def from_near(buf, recv, turn):
        for side in range(CORES):
            remote(buf.at[side], buf.at[side], near_send.at[turn, 0], recv.at[side], k, partner).wait_recv()

    p_copy = to_pair(p_buf.at[core], p_buf.at[core], 0)
    p_copy.start()
    f_copies = to_near(f_buf, fn_buf.at[core], fn_recv.at[core], 0)
    u_copies = to_near(gauge_ref.at[core], un_buf.at[core], un_recv.at[core], 1)
    for copy in f_copies:
        copy.start()

    def got_pair(dst, turn):
        remote(dst, dst, pair_send.at[turn], pair_recv.at[turn], k, partner).wait_recv()

    got_pair(p_buf.at[1 - core], 0)

    def stacked(buf):
        flat = buf[...].reshape(CORES * 2 * rows, nb)
        turned = []
        for side in range(CORES):
            turned += [buf[side, 1], -buf[side, 0]]
        return flat, jnp.concatenate(turned, axis=0)

    own_flat, own_turned = stacked(p_buf)
    a_full[...] = mm_t(own_flat, own_flat) + mm_t(own_flat, own_turned)
    for i in range(A_CHUNKS):
        local[i] = a_full[pl.ds(pl.multiple_of(core * half + i * chunk, 8), chunk), :]

    def relay_one(i):
        owner = low + lax.rem(i, 2) if line > 1 else 0

        @pl.when(q < owner)
        def _():
            @pl.when(q > 0)
            def _():
                remote(r_buf.at[i], r_buf.at[i], red_send.at[i], red_recv_r.at[i], k, partner).wait_recv()

            s_buf[i] = (local[i] + r_buf[i].astype(F32)).astype(BF16)
            remote(s_buf.at[i], r_buf.at[i], red_send.at[i], red_recv_r.at[i], k, p + CORES).start()

        @pl.when(q > owner)
        def _():
            @pl.when(q < line - 1)
            def _():
                remote(l_buf.at[i], l_buf.at[i], red_send.at[i], red_recv_l.at[i], k, partner).wait_recv()

            s_buf[i] = (local[i] + l_buf[i].astype(F32)).astype(BF16)
            remote(s_buf.at[i], l_buf.at[i], red_send.at[i], red_recv_l.at[i], k, p - CORES).start()

    def total_one(i):
        owner = low + lax.rem(i, 2) if line > 1 else 0

        @pl.when(q == owner)
        def _():
            @pl.when(q > 0)
            def _():
                remote(r_buf.at[i], r_buf.at[i], red_send.at[i], red_recv_r.at[i], k, partner).wait_recv()

            @pl.when(q < line - 1)
            def _():
                remote(l_buf.at[i], l_buf.at[i], red_send.at[i], red_recv_l.at[i], k, partner).wait_recv()

            t_buf[i] = (local[i] + r_buf[i].astype(F32) + l_buf[i].astype(F32)).astype(BF16)

            @pl.when(q > 0)
            def _():
                remote(t_buf.at[i], t_buf.at[i], cast_send.at[0, i], tot_recv.at[i], k, p - CORES).start()

            @pl.when(q < line - 1)
            def _():
                remote(t_buf.at[i], t_buf.at[i], cast_send.at[1, i], tot_recv.at[i], k, p + CORES).start()

    def cast_one(i):
        owner = low + lax.rem(i, 2) if line > 1 else 0

        @pl.when(q != owner)
        def _():
            remote(t_buf.at[i], t_buf.at[i], cast_send.at[0, i], tot_recv.at[i], k, partner).wait_recv()

        @pl.when((q < owner) & (q > 0))
        def _():
            remote(t_buf.at[i], t_buf.at[i], cast_send.at[0, i], tot_recv.at[i], k, p - CORES).start()

        @pl.when((q > owner) & (q < line - 1))
        def _():
            remote(t_buf.at[i], t_buf.at[i], cast_send.at[1, i], tot_recv.at[i], k, p + CORES).start()

    def settle_one(i):
        owner = low + lax.rem(i, 2) if line > 1 else 0

        @pl.when(q != owner)
        def _():
            remote(s_buf.at[i], s_buf.at[i], red_send.at[i], tot_recv.at[i], k, partner).wait_send()

        @pl.when((q <= owner) & (q > 0))
        def _():
            remote(t_buf.at[i], t_buf.at[i], cast_send.at[0, i], tot_recv.at[i], k, partner).wait_send()

        @pl.when((q >= owner) & (q < line - 1))
        def _():
            remote(t_buf.at[i], t_buf.at[i], cast_send.at[1, i], tot_recv.at[i], k, partner).wait_send()

    def over_pairs(one, first, last):
        def step(i, carry):
            one(i)
            return carry

        lax.fori_loop(2 * first, 2 * last, step, 0)

    outer = (q == 0) | (q == line - 1)
    inner = jnp.logical_not(outer)

    def cross_terms():
        from_near(fn_buf, fn_recv, 0)
        near_flat, near_turned = stacked(fn_buf)
        for part, right in enumerate((near_flat, near_turned)):
            cross = mm_t(own_flat, right)
            for j in range(c_chunks):
                local[A_CHUNKS + 2 * j + part] = cross[j * chunk : (j + 1) * chunk]

    over_pairs(relay_one, 0, pairs_a)
    over_pairs(total_one, 0, pairs_a)

    @pl.when(outer)
    def _():
        cross_terms()
        over_pairs(relay_one, pairs_a, pairs_all)

    over_pairs(cast_one, 0, pairs_a)

    mine = pl.ds(0, A_CHUNKS)
    a_copy = to_pair(t_buf.at[mine], a_other, 1)
    a_copy.start()

    @pl.when(inner)
    def _():
        cross_terms()

    for copy in u_copies:
        copy.start()

    def sums(j, carry):
        @pl.when(inner & (j < pairs_all))
        def _():
            over_pairs(relay_one, j, j + 1)

        @pl.when((j >= pairs_a + TOTAL_LAG) & (j < pairs_all + TOTAL_LAG))
        def _():
            over_pairs(total_one, j - TOTAL_LAG, j - TOTAL_LAG + 1)

        @pl.when(j >= pairs_a + CAST_LAG)
        def _():
            over_pairs(cast_one, j - CAST_LAG, j - CAST_LAG + 1)

        return carry

    lax.fori_loop(pairs_a, early, sums, 0)
    got_pair(a_other, 1)
    a_full[pl.ds(pl.multiple_of(core * half, 8), half), :] = (
        t_buf[mine].astype(F32).reshape(half, nb)
    )
    a_full[pl.ds(pl.multiple_of((1 - core) * half, 8), half), :] = (
        a_other[...].astype(F32).reshape(half, nb)
    )

    eye = (
        lax.broadcasted_iota(jnp.int32, (nb, nb), 0) == lax.broadcasted_iota(jnp.int32, (nb, nb), 1)
    ).astype(F32)
    packed = a_full[...]
    scale = 2.0 * jnp.sum(packed * eye) / nb
    e_re, e_im = halves(packed / scale - 0.5 * eye)
    e_re_b, e_im_b = e_re.astype(BF16), e_im.astype(BF16)
    sq_re, sq_im = complex_mm(e_re_b, e_im_b, e_re_b, e_im_b)
    left_re, left_im = e_re - 0.5 * sq_re, e_im - 0.5 * sq_im
    right_re, right_im = 0.25 * sq_re - 1.25 * e_re, 0.25 * sq_im - 1.25 * e_im
    last_re, last_im = complex_mm(
        left_re.astype(BF16), left_im.astype(BF16), right_re.astype(BF16), right_im.astype(BF16)
    )
    white_re = 1.38671875 * eye - 0.75 * e_re - 0.78125 * left_re - 0.3125 * right_re - 0.5 * last_re
    white_im = -0.75 * e_im - 0.78125 * left_im - 0.3125 * right_im - 0.5 * last_im
    w_buf[...] = (white_re + white_im).astype(BF16).reshape(CORES, half, nb)
    w_copies = to_near(w_buf.at[core], wn_buf.at[core], wn_recv.at[core], 2)
    for copy in w_copies:
        copy.start()
    w_re, w_im = white_re.astype(BF16), white_im.astype(BF16)

    out_re, out_im = complex_mm(f_buf[0], f_buf[1], w_re, w_im)
    white_out[0] = out_re.astype(BF16)
    white_out[1] = out_im.astype(BF16)
    v_re, v_im = complex_mm(w_re, w_im, gauge_ref[0], gauge_ref[1])
    v_buf[0] = v_re.astype(BF16)
    v_buf[1] = v_im.astype(BF16)

    lax.fori_loop(early, pairs_all + CAST_LAG, sums, 0)
    from_near(un_buf, un_recv, 1)
    from_near(wn_buf, wn_recv, 2)
    next_re, next_im = halves(wn_buf[...].astype(F32).reshape(nb, nb))
    vn_re, vn_im = complex_mm(next_re.astype(BF16), next_im.astype(BF16), un_buf[0], un_buf[1])
    cross_re, cross_im = (
        jnp.concatenate([t_buf[A_CHUNKS + 2 * j + part] for j in range(c_chunks)], axis=0)
        for part in range(2)
    )
    x_re, x_im = complex_mm(cross_re, cross_im, vn_re.astype(BF16), vn_im.astype(BF16))
    x_re, x_im = x_re.astype(BF16), x_im.astype(BF16)
    root = math.sqrt(rows * pw_count)
    corr_re = mm_t(v_buf[0], x_re) + mm_t(v_buf[1], x_im)
    corr_im = mm_t(v_buf[0], x_im) - mm_t(v_buf[1], x_re)
    c_buf[core, 0] = (corr_re * root).astype(BF16)
    c_buf[core, 1] = (corr_im * root).astype(BF16)
    c_copy = to_pair(c_buf.at[core], c_buf.at[core], 2)
    c_copy.start()

    for copy in (p_copy, a_copy) + f_copies + u_copies + w_copies:
        copy.wait_send()

    def settle(i, carry):
        settle_one(i)
        return carry

    lax.fori_loop(0, 2 * pairs_all, settle, 0)
    got_pair(c_buf.at[1 - core], 2)
    corr_out[...] = c_buf[...]
    c_copy.wait_send()


def on_device(ka_count, pw_count, band_coeffs, cutoff_weight, row_order, neighbour, gauge_matrix):
    rows, nb = band_coeffs.shape[2], band_coeffs.shape[3]
    half = nb // CORES
    chunk = half // A_CHUNKS
    total = A_CHUNKS + 2 * (nb // chunk)
    vmem = pl.BlockSpec(memory_space=pltpu.VMEM)
    dma = pltpu.SemaphoreType.DMA
    whitened, pair = pl.pallas_call(
        functools.partial(kernel, ka_count, pw_count),
        out_shape=(
            jax.ShapeDtypeStruct((2, rows, nb), BF16),
            jax.ShapeDtypeStruct((2, 2, nb, nb), BF16),
        ),
        in_specs=[vmem] * 4,
        out_specs=(vmem, vmem),
        scratch_shapes=[
            pltpu.VMEM((2, rows, nb), BF16),
            pltpu.VMEM((CORES, 2, rows, nb), BF16),
            pltpu.VMEM((CORES, 2, rows, nb), BF16),
            pltpu.VMEM((2, nb, nb), BF16),
            pltpu.VMEM((nb, nb), F32),
            pltpu.VMEM((total, chunk, nb), F32),
            pltpu.VMEM((total, chunk, nb), BF16),
            pltpu.VMEM((total, chunk, nb), BF16),
            pltpu.VMEM((total, chunk, nb), BF16),
            pltpu.VMEM((total, chunk, nb), BF16),
            pltpu.VMEM((A_CHUNKS, chunk, nb), BF16),
            pltpu.VMEM((CORES, half, nb), BF16),
            pltpu.VMEM((CORES, half, nb), BF16),
            pltpu.VMEM((2, nb, nb), BF16),
            pltpu.VMEM((2, 2, nb, nb), BF16),
            dma((3,)),
            dma((3,)),
            dma((3, 2)),
            dma((2,)),
            dma((2,)),
            dma((2,)),
            dma((total,)),
            dma((total,)),
            dma((total,)),
            dma((total,)),
            dma((2, total)),
        ],
        compiler_params=pltpu.CompilerParams(collective_id=0, has_side_effects=True),
    )(band_coeffs[0], cutoff_weight, row_order, gauge_matrix[0])
    group = lax.axis_index("ka")
    looks_ahead = neighbour[0] == (group + 1) % ka_count
    correlations = jnp.where(looks_ahead, pair, pair[::-1]).astype(F32)
    return (whitened[None], correlations[None])


def solution(mesh):
    in_specs = (
        P("ka", None, "pw", None),
        P("ka", "pw"),
        P("ka", "pw"),
        P("ka"),
        P("ka", None, None, None),
    )
    out_specs = (P("ka", None, "pw", None), P("ka", None, None, None, None))
    return jax.shard_map(
        functools.partial(on_device, mesh.shape["ka"], mesh.shape["pw"]),
        mesh=mesh, in_specs=in_specs, out_specs=out_specs, check_vma=False,
    )
```

```python
import functools
import math

import jax
import jax.numpy as jnp
from jax import lax
from jax.experimental import pallas as pl
from jax.experimental.pallas import tpu as pltpu
from jax.sharding import PartitionSpec as P

MESH = pl.DeviceIdType.MESH
CORES = 2
A_CHUNKS = 4
EARLY = 3
LATE = 3
TOTAL_LAG = 3
CAST_LAG = 6
F32 = jnp.float32
BF16 = jnp.bfloat16


def mm(left, right):
    return jnp.dot(left, right, preferred_element_type=F32)


def mm_t(left, right):
    return lax.dot_general(left, right, (((0,), (0,)), ((), ())), preferred_element_type=F32)


def complex_mm(left_re, left_im, right_re, right_im):
    real_part = mm(left_re, right_re) - mm(left_im, right_im)
    imag_part = mm(left_re, right_im) + mm(left_im, right_re)
    return real_part, imag_part


def halves(packed):
    turned = packed.T
    return 0.5 * (packed + turned), 0.5 * (packed - turned)


def kernel(
    ka_count,
    pw_count,
    bands_ref,
    weight_ref,
    order_ref,
    gauge_ref,
    white_out,
    corr_out,
    f_buf,
    p_buf,
    fn_buf,
    un_buf,
    a_full,
    local,
    r_buf,
    l_buf,
    s_buf,
    t_buf,
    a_other,
    w_buf,
    wn_buf,
    v_buf,
    c_buf,
    pair_send,
    pair_recv,
    near_send,
    fn_recv,
    un_recv,
    wn_recv,
    red_send,
    red_recv_r,
    red_recv_l,
    tot_recv,
    cast_send,
):
    rows, nb = bands_ref.shape[1], bands_ref.shape[2]
    half = nb // CORES
    chunk = half // A_CHUNKS
    c_chunks = nb // chunk
    pairs_a = A_CHUNKS // 2
    pairs_all = (A_CHUNKS + 2 * c_chunks) // 2
    early = pairs_a + EARLY
    k = lax.axis_index("ka")
    p = lax.axis_index("pw")
    core = lax.rem(p, CORES)
    q = lax.div(p, CORES)
    line = pw_count // CORES
    low = (line - 1) // 2
    ahead = lax.rem(k + 1, ka_count)
    behind = lax.rem(k + ka_count - 1, ka_count)
    base = q * CORES
    partner = base + 1 - core

    barrier = pltpu.get_barrier_semaphore()

    def greet(a, b):
        pl.semaphore_signal(barrier, inc=1, device_id=(a, b), device_id_type=MESH)

    greet(k, partner)
    for other in (ahead, behind):
        for side in range(CORES):
            greet(other, base + side)

    @pl.when(q > 0)
    def _():
        greet(k, p - CORES)

    @pl.when(q < line - 1)
    def _():
        greet(k, p + CORES)

    eye = (
        lax.broadcasted_iota(jnp.int32, (nb, nb), 0) == lax.broadcasted_iota(jnp.int32, (nb, nb), 1)
    ).astype(F32)
    first = lax.broadcasted_iota(jnp.int32, (nb, nb), 0) == 0
    rest = jnp.where(first, 0.0, eye)

    row_id = lax.broadcasted_iota(jnp.int32, (rows, rows), 0)
    col_id = lax.broadcasted_iota(jnp.int32, (rows, rows), 1)
    weight = jnp.sum(jnp.where(row_id == col_id, weight_ref[...], 0.0), axis=1, keepdims=True)
    pick = (row_id == order_ref[...] - p * rows).astype(BF16)
    for part in range(2):
        filtered = (bands_ref[part].astype(F32) * weight).astype(BF16)
        f_buf[part] = filtered
        p_buf[core, part] = mm(pick, filtered).astype(BF16)

    @pl.when(q == 0)
    def _():
        r_buf[...] = jnp.zeros_like(r_buf)

    @pl.when(q == line - 1)
    def _():
        l_buf[...] = jnp.zeros_like(l_buf)

    pl.semaphore_wait(barrier, 5 + (q > 0).astype(jnp.int32) + (q < line - 1).astype(jnp.int32))

    def remote(src, dst, send, recv, a, b):
        return pltpu.make_async_remote_copy(
            src_ref=src, dst_ref=dst, send_sem=send, recv_sem=recv,
            device_id=(a, b), device_id_type=MESH,
        )

    def to_pair(src, dst, turn):
        return remote(src, dst, pair_send.at[turn], pair_recv.at[turn], k, partner)

    def to_near(src, dst, recv, turn):
        return (
            remote(src, dst, near_send.at[turn, 0], recv, behind, base),
            remote(src, dst, near_send.at[turn, 1], recv, ahead, base + 1),
        )

    def from_near(buf, recv, turn):
        for side in range(CORES):
            remote(buf.at[side], buf.at[side], near_send.at[turn, 0], recv.at[side], k, partner).wait_recv()

    p_copy = to_pair(p_buf.at[core], p_buf.at[core], 0)
    p_copy.start()
    f_copies = to_near(f_buf, fn_buf.at[core], fn_recv.at[core], 0)
    u_copies = to_near(gauge_ref.at[core], un_buf.at[core], un_recv.at[core], 1)
    even = lax.rem(k, 2) == 0

    @pl.when(even)
    def _():
        f_copies[1].start()
        f_copies[0].start()

    @pl.when(jnp.logical_not(even))
    def _():
        f_copies[0].start()
        f_copies[1].start()

    for copy in u_copies:
        copy.start()


    def got_pair(dst, turn):
        remote(dst, dst, pair_send.at[turn], pair_recv.at[turn], k, partner).wait_recv()

    got_pair(p_buf.at[1 - core], 0)

    def stacked(buf):
        flat = buf[...].reshape(CORES * 2 * rows, nb)
        turned = []
        for side in range(CORES):
            turned += [buf[side, 1], -buf[side, 0]]
        return flat, jnp.concatenate(turned, axis=0)

    own_flat, own_turned = stacked(p_buf)
    gram = mm_t(own_flat, own_flat) + mm_t(own_flat, own_turned)
    a_full[...] = gram - (jnp.sum(gram * eye) / nb) * rest
    for i in range(A_CHUNKS):
        local[i] = a_full[pl.ds(pl.multiple_of(core * half + i * chunk, 8), chunk), :]

    def relay_one(i):
        owner = low + lax.rem(i, 2) if line > 1 else 0

        @pl.when(q < owner)
        def _():
            @pl.when(q > 0)
            def _():
                remote(r_buf.at[i], r_buf.at[i], red_send.at[i], red_recv_r.at[i], k, partner).wait_recv()

            s_buf[i] = (local[i] + r_buf[i].astype(F32)).astype(BF16)
            remote(s_buf.at[i], r_buf.at[i], red_send.at[i], red_recv_r.at[i], k, p + CORES).start()

        @pl.when(q > owner)
        def _():
            @pl.when(q < line - 1)
            def _():
                remote(l_buf.at[i], l_buf.at[i], red_send.at[i], red_recv_l.at[i], k, partner).wait_recv()

            s_buf[i] = (local[i] + l_buf[i].astype(F32)).astype(BF16)
            remote(s_buf.at[i], l_buf.at[i], red_send.at[i], red_recv_l.at[i], k, p - CORES).start()

    def total_one(i):
        owner = low + lax.rem(i, 2) if line > 1 else 0

        @pl.when(q == owner)
        def _():
            @pl.when(q > 0)
            def _():
                remote(r_buf.at[i], r_buf.at[i], red_send.at[i], red_recv_r.at[i], k, partner).wait_recv()

            @pl.when(q < line - 1)
            def _():
                remote(l_buf.at[i], l_buf.at[i], red_send.at[i], red_recv_l.at[i], k, partner).wait_recv()

            t_buf[i] = (local[i] + r_buf[i].astype(F32) + l_buf[i].astype(F32)).astype(BF16)

            @pl.when(q > 0)
            def _():
                remote(t_buf.at[i], t_buf.at[i], cast_send.at[0, i], tot_recv.at[i], k, p - CORES).start()

            @pl.when(q < line - 1)
            def _():
                remote(t_buf.at[i], t_buf.at[i], cast_send.at[1, i], tot_recv.at[i], k, p + CORES).start()

    def cast_one(i):
        owner = low + lax.rem(i, 2) if line > 1 else 0

        @pl.when(q != owner)
        def _():
            remote(t_buf.at[i], t_buf.at[i], cast_send.at[0, i], tot_recv.at[i], k, partner).wait_recv()

        @pl.when((q < owner) & (q > 0))
        def _():
            remote(t_buf.at[i], t_buf.at[i], cast_send.at[0, i], tot_recv.at[i], k, p - CORES).start()

        @pl.when((q > owner) & (q < line - 1))
        def _():
            remote(t_buf.at[i], t_buf.at[i], cast_send.at[1, i], tot_recv.at[i], k, p + CORES).start()

    def settle_one(i):
        owner = low + lax.rem(i, 2) if line > 1 else 0

        @pl.when(q != owner)
        def _():
            remote(s_buf.at[i], s_buf.at[i], red_send.at[i], tot_recv.at[i], k, partner).wait_send()

        @pl.when((q <= owner) & (q > 0))
        def _():
            remote(t_buf.at[i], t_buf.at[i], cast_send.at[0, i], tot_recv.at[i], k, partner).wait_send()

        @pl.when((q >= owner) & (q < line - 1))
        def _():
            remote(t_buf.at[i], t_buf.at[i], cast_send.at[1, i], tot_recv.at[i], k, partner).wait_send()

    def over_pairs(one, first, last):
        def step(i, carry):
            one(i)
            return carry

        lax.fori_loop(2 * first, 2 * last, step, 0)

    outer = (q == 0) | (q == line - 1)
    inner = jnp.logical_not(outer)

    def cross_terms():
        from_near(fn_buf, fn_recv, 0)
        near_flat, near_turned = stacked(fn_buf)
        for part, right in enumerate((near_flat, near_turned)):
            cross = mm_t(own_flat, right)
            for j in range(c_chunks):
                local[A_CHUNKS + 2 * j + part] = cross[j * chunk : (j + 1) * chunk]

    over_pairs(relay_one, 0, pairs_a)
    over_pairs(total_one, 0, pairs_a)

    @pl.when(outer)
    def _():
        cross_terms()
        over_pairs(relay_one, pairs_a, pairs_all)

    over_pairs(cast_one, 0, pairs_a)

    mine = pl.ds(0, A_CHUNKS)
    a_copy = to_pair(t_buf.at[mine], a_other, 1)
    a_copy.start()

    @pl.when(inner)
    def _():
        cross_terms()

    def sums(j, carry):
        @pl.when(inner & (j < pairs_all))
        def _():
            over_pairs(relay_one, j, j + 1)

        @pl.when((j >= pairs_a + TOTAL_LAG) & (j < pairs_all + TOTAL_LAG))
        def _():
            over_pairs(total_one, j - TOTAL_LAG, j - TOTAL_LAG + 1)

        @pl.when(j >= pairs_a + CAST_LAG)
        def _():
            over_pairs(cast_one, j - CAST_LAG, j - CAST_LAG + 1)

        return carry

    lax.fori_loop(pairs_a, early, sums, 0)
    got_pair(a_other, 1)
    a_full[pl.ds(pl.multiple_of(core * half, 8), half), :] = (
        t_buf[mine].astype(F32).reshape(half, nb)
    )
    a_full[pl.ds(pl.multiple_of((1 - core) * half, 8), half), :] = (
        a_other[...].astype(F32).reshape(half, nb)
    )

    packed = a_full[...]
    mean = jnp.sum(packed * eye)
    deviation = packed - mean * (eye - rest)
    e_re, e_im = halves(deviation / (2.0 * mean))
    e_re_b, e_im_b = e_re.astype(BF16), e_im.astype(BF16)
    sq_re, sq_im = complex_mm(e_re_b, e_im_b, e_re_b, e_im_b)
    lax.fori_loop(early, early + 2, sums, 0)
    left_re, left_im = e_re - 0.5 * sq_re, e_im - 0.5 * sq_im
    right_re, right_im = 0.25 * sq_re - 1.25 * e_re, 0.25 * sq_im - 1.25 * e_im
    last_re, last_im = complex_mm(
        left_re.astype(BF16), left_im.astype(BF16), right_re.astype(BF16), right_im.astype(BF16)
    )
    white_re = 1.38671875 * eye - 0.75 * e_re - 0.78125 * left_re - 0.3125 * right_re - 0.5 * last_re
    white_im = -0.75 * e_im - 0.78125 * left_im - 0.3125 * right_im - 0.5 * last_im
    w_buf[...] = (white_re + white_im).astype(BF16).reshape(CORES, half, nb)
    w_copies = to_near(w_buf.at[core], wn_buf.at[core], wn_recv.at[core], 2)
    for copy in w_copies:
        copy.start()
    w_re, w_im = white_re.astype(BF16), white_im.astype(BF16)

    lax.fori_loop(early + 2, early + 5, sums, 0)
    out_re, out_im = complex_mm(f_buf[0], f_buf[1], w_re, w_im)
    white_out[0] = out_re.astype(BF16)
    white_out[1] = out_im.astype(BF16)
    v_re, v_im = complex_mm(w_re, w_im, gauge_ref[0], gauge_ref[1])
    v_buf[0] = v_re.astype(BF16)
    v_buf[1] = v_im.astype(BF16)

    lax.fori_loop(early + 5, pairs_all + CAST_LAG - LATE, sums, 0)
    from_near(un_buf, un_recv, 1)
    from_near(wn_buf, wn_recv, 2)
    next_re, next_im = halves(wn_buf[...].astype(F32).reshape(nb, nb))
    vn_re, vn_im = complex_mm(next_re.astype(BF16), next_im.astype(BF16), un_buf[0], un_buf[1])
    lax.fori_loop(pairs_all + CAST_LAG - LATE, pairs_all + CAST_LAG, sums, 0)
    cross_re, cross_im = (
        jnp.concatenate([t_buf[A_CHUNKS + 2 * j + part] for j in range(c_chunks)], axis=0)
        for part in range(2)
    )
    x_re, x_im = complex_mm(cross_re, cross_im, vn_re.astype(BF16), vn_im.astype(BF16))
    x_re, x_im = x_re.astype(BF16), x_im.astype(BF16)
    root = math.sqrt(rows * pw_count)
    corr_re = mm_t(v_buf[0], x_re) + mm_t(v_buf[1], x_im)
    corr_im = mm_t(v_buf[0], x_im) - mm_t(v_buf[1], x_re)
    c_buf[core, 0] = (corr_re * root).astype(BF16)
    c_buf[core, 1] = (corr_im * root).astype(BF16)
    c_copy = to_pair(c_buf.at[core], c_buf.at[core], 2)
    c_copy.start()

    for copy in (p_copy, a_copy) + f_copies + u_copies + w_copies:
        copy.wait_send()

    def settle(i, carry):
        settle_one(i)
        return carry

    lax.fori_loop(0, 2 * pairs_all, settle, 0)
    got_pair(c_buf.at[1 - core], 2)
    corr_out[...] = c_buf[...]
    c_copy.wait_send()


def on_device(ka_count, pw_count, band_coeffs, cutoff_weight, row_order, neighbour, gauge_matrix):
    rows, nb = band_coeffs.shape[2], band_coeffs.shape[3]
    half = nb // CORES
    chunk = half // A_CHUNKS
    total = A_CHUNKS + 2 * (nb // chunk)
    vmem = pl.BlockSpec(memory_space=pltpu.VMEM)
    dma = pltpu.SemaphoreType.DMA
    whitened, pair = pl.pallas_call(
        functools.partial(kernel, ka_count, pw_count),
        out_shape=(
            jax.ShapeDtypeStruct((2, rows, nb), BF16),
            jax.ShapeDtypeStruct((2, 2, nb, nb), BF16),
        ),
        in_specs=[vmem] * 4,
        out_specs=(vmem, vmem),
        scratch_shapes=[
            pltpu.VMEM((2, rows, nb), BF16),
            pltpu.VMEM((CORES, 2, rows, nb), BF16),
            pltpu.VMEM((CORES, 2, rows, nb), BF16),
            pltpu.VMEM((2, nb, nb), BF16),
            pltpu.VMEM((nb, nb), F32),
            pltpu.VMEM((total, chunk, nb), F32),
            pltpu.VMEM((total, chunk, nb), BF16),
            pltpu.VMEM((total, chunk, nb), BF16),
            pltpu.VMEM((total, chunk, nb), BF16),
            pltpu.VMEM((total, chunk, nb), BF16),
            pltpu.VMEM((A_CHUNKS, chunk, nb), BF16),
            pltpu.VMEM((CORES, half, nb), BF16),
            pltpu.VMEM((CORES, half, nb), BF16),
            pltpu.VMEM((2, nb, nb), BF16),
            pltpu.VMEM((2, 2, nb, nb), BF16),
            dma((3,)),
            dma((3,)),
            dma((3, 2)),
            dma((2,)),
            dma((2,)),
            dma((2,)),
            dma((total,)),
            dma((total,)),
            dma((total,)),
            dma((total,)),
            dma((2, total)),
        ],
        compiler_params=pltpu.CompilerParams(collective_id=0, has_side_effects=True),
    )(band_coeffs[0], cutoff_weight, row_order, gauge_matrix[0])
    group = lax.axis_index("ka")
    looks_ahead = neighbour[0] == (group + 1) % ka_count
    correlations = jnp.stack(
        [jnp.where(looks_ahead, pair[0], pair[1]), jnp.where(looks_ahead, pair[1], pair[0])]
    ).astype(F32)
    return (whitened[None], correlations[None])


def solution(mesh):
    in_specs = (
        P("ka", None, "pw", None),
        P("ka", "pw"),
        P("ka", "pw"),
        P("ka"),
        P("ka", None, None, None),
    )
    out_specs = (P("ka", None, "pw", None), P("ka", None, None, None, None))
    return jax.shard_map(
        functools.partial(on_device, mesh.shape["ka"], mesh.shape["pw"]),
        mesh=mesh, in_specs=in_specs, out_specs=out_specs, check_vma=False,
    )
```
